512 devices in a mesh: seq: 64 (over z, y), mp: 8 (over x, core).
Axes of the slice: x: 4, y: 8, z: 8, core: 2. Of those that a mesh axis runs over, the one named last changes fastest.
Arguments:
- query: bfloat16 [16384, 3072], P('seq', 'mp'), may hold values from -4.5 to 4.5
- key: bfloat16 [16384, 3072], P('seq', 'mp'), may hold values from -4.5 to 4.5
- value: bfloat16 [16384, 3072], P('seq', 'mp'), may hold values from -6 to 6
- clip_lengths: int32 [4, 4], replicated, may hold values from 0 to 4096, as said below
Outputs:
- attended: bfloat16 [16384, 3072], P(('seq', 'mp'))
The draws below stay inside these ranges and needn't reach their ends.
Inputs may be any that keep to these rules, and one draw needn't show every extreme that they name: `clip_lengths`: each row sums to 4096; a clip slot may be empty; in some bucket one clip fills all 4096 tokens.
All inputs are finite; a program needn't handle non-finite values.
Results may differ from the reference program's by a relative error of at most 0.01.
Values may be sent and summed in bfloat16 or wider, within the bound.
No kernel may reach another device: no remote copies, remote signals or barrier semaphores. Data moves between devices by JAX's collectives and lax.ppermute only.
A program may use at most 64 MiB of HBM per device.

```python
import jax
import jax.numpy as jnp
from jax import lax

HD = 128
PER = 4
D = 3072
MOST = 4096
BUCKETS = 4
TOKENS = 16384


def draw_query(key, part):
    base = jax.random.normal(jax.random.fold_in(key, 1), (TOKENS, D), jnp.float32)
    return jnp.clip(base, -4.5, 4.5).astype(jnp.bfloat16)


def draw_key(key, part):
    base = jax.random.normal(jax.random.fold_in(key, 2), (TOKENS, D), jnp.float32)
    return jnp.clip(base, -4.5, 4.5).astype(jnp.bfloat16)


def draw_clip_lengths(key, part):
    cuts = jax.random.randint(jax.random.fold_in(key, 21), (BUCKETS, PER - 1), 0, MOST + 1).astype(jnp.int32)
    cuts = jnp.sort(cuts, axis=1)
    zeros = jnp.zeros((BUCKETS, 1), jnp.int32)
    filled = jnp.full((BUCKETS, 1), MOST, jnp.int32)
    lengths = jnp.diff(jnp.concatenate([zeros, cuts, filled], axis=1), axis=1)
    chosen = jax.random.randint(jax.random.fold_in(key, 22), (), 0, BUCKETS).astype(jnp.int32)
    single = jnp.concatenate([filled, jnp.zeros((BUCKETS, PER - 1), jnp.int32)], axis=1)
    rows = jnp.arange(BUCKETS, dtype=jnp.int32)[:, None] == chosen
    return jnp.where(rows, single, lengths).astype(jnp.int32)


def level_of(stream_key, shape, shards, smallest, largest):
    def one(dim, parts):
        draws = jax.random.uniform(jax.random.fold_in(jax.random.fold_in(stream_key, 6), dim), (parts,), jnp.float32, smallest / len(shards), largest / len(shards))
        return jnp.repeat(jnp.exp(draws), shape[dim] // parts).reshape((-1,) + (1,) * (len(shape) - dim - 1))

    loudness = one(*shards[0])
    for cut in shards[1:]:
        loudness = loudness * one(*cut)
    return loudness


def noise(rng, extent, spread, limit, split=(), kind=jnp.bfloat16):
    drawn = jax.random.normal(rng, extent, jnp.float32) * spread
    if len(split) > 0:
        drawn = level_of(rng, extent, split, -0.22, 0.18) * drawn
    return jnp.clip(drawn, min=-limit, max=limit).astype(kind)


def setup_inputs(seed: int = 0) -> dict:
    key_list = jax.random.split(jax.random.key(seed), 5)
    return {
        "query": draw_query(jax.random.fold_in(key_list[4], 71), 0),
        "key": draw_key(jax.random.fold_in(key_list[4], 71), 0),
        "value": noise(key_list[2], (TOKENS, D), 1.0, 6.0, ((0, 64), (1, 8))),
        "clip_lengths": draw_clip_lengths(jax.random.fold_in(key_list[4], 71), 0),
    }


NEG = -1.0e30


def clip_of(places, ends):
    bucket = (places // MOST).astype(jnp.int32)
    offset = (places - bucket * MOST).astype(jnp.int32)
    hits = jnp.sum((offset[:, None, None] >= ends[None, :, :]).astype(jnp.int32), axis=2).astype(jnp.int32)
    pick = bucket[:, None] == jnp.arange(BUCKETS, dtype=jnp.int32)[None, :]
    inner = jnp.sum(jnp.where(pick, hits, 0), axis=1).astype(jnp.int32)
    return (bucket * PER + inner).astype(jnp.int32)


def reference(query, key, value, clip_lengths):
    heads = D // HD
    scale = 1.0 / (HD ** 0.5)
    ends = jnp.cumsum(clip_lengths, axis=1).astype(jnp.int32)
    clip_ids = clip_of(jnp.arange(TOKENS, dtype=jnp.int32), ends)
    block = min(512, MOST)
    outputs = []
    for bucket in range(BUCKETS):
        low = bucket * MOST
        k_part = key[low:low + MOST].reshape(MOST, heads, HD).astype(jnp.float32)
        v_part = value[low:low + MOST].reshape(MOST, heads, HD).astype(jnp.float32)
        k_ids = clip_ids[low:low + MOST]
        q_all = query[low:low + MOST].reshape(MOST // block, block, heads, HD)
        q_idx = k_ids.reshape(MOST // block, block)

        def one_block(items):
            q_part, q_ids = items
            score = jnp.einsum("qhd,khd->hqk", q_part.astype(jnp.float32), k_part,
                               precision=lax.Precision.HIGHEST) * scale
            keep = (q_ids[:, None] == k_ids[None, :])[None]
            score = jnp.where(keep, score, NEG)
            top = jnp.max(score, axis=-1, keepdims=True)
            weight = jnp.where(keep, jnp.exp(score - top), 0.0)
            total = jnp.sum(weight, axis=-1)
            weight_low = lax.optimization_barrier(weight.astype(jnp.bfloat16)).astype(jnp.float32)
            summed = jnp.einsum("hqk,khd->qhd", weight_low, v_part, precision=lax.Precision.HIGHEST)
            result = summed / jnp.transpose(total)[:, :, None]
            return result.reshape(block, D).astype(jnp.bfloat16)

        pieces = lax.map(one_block, (q_all, q_idx))
        outputs.append(pieces.reshape(MOST, D))
    return jnp.concatenate(outputs, axis=0)
```

```python
import jax
import jax.numpy as jnp
from jax import lax
from jax.experimental import pallas as pl
from jax.experimental.pallas import tpu as pltpu
from jax.sharding import Mesh, PartitionSpec as P

HD = 128
HEADS = 3
ROWS = 256
SPAN = 4096
WIDTH = HEADS * HD
SENT = WIDTH + HD
SCALE2 = 1.4426950408889634 / HD**0.5
NEG = -1e30
LOW = -1e20


def clip_at(place, ends):
    return sum((place >= e).astype(jnp.int32) for e in ends)


def attend_kernel(place_ref, lengths_ref, q_own, q_other, *refs):
    kv_refs = refs[:7]
    far_key, far_value, out_ref, score_ref = refs[7:]
    bucket, z, y = place_ref[0], place_ref[1], place_ref[2]
    ends = []
    running = jnp.int32(0)
    for slot in range(3):
        running = running + lengths_ref[bucket, slot]
        ends.append(running)
    key_parts = [(r, 0) for r in kv_refs] + [(far_key, 0)]
    value_parts = [(r, ROWS) for r in kv_refs] + [(far_value, 0)]
    shifts = (0, -1, 1, -2, 2, -3, 3, 4)
    key_starts = [z * (SPAN // 2) + ((y + s) & 7) * ROWS for s in shifts]
    q_starts = [z * (SPAN // 2) + y * ROWS, (1 - z) * (SPAN // 2) + y * ROWS]
    first = clip_at(z * (SPAN // 2), ends)
    same = first == clip_at(z * (SPAN // 2) + SPAN // 2 - 1, ends)
    for q0 in q_starts:
        same &= first == clip_at(q0, ends)
        same &= first == clip_at(q0 + ROWS - 1, ends)

    def body(masked):
        ones = jnp.ones((ROWS, HD), jnp.bfloat16)
        for turn, (q_ref, q0) in enumerate(zip((q_own, q_other), q_starts)):
            row0 = pl.multiple_of((z if turn == 0 else 1 - z) * ROWS, ROWS)
            logs = []
            if masked:
                q_ids = clip_at(q0 + lax.broadcasted_iota(jnp.int32, (ROWS, 1), 0), ends)
            for h in range(HEADS):
                cols = slice(h * HD, (h + 1) * HD)
                buf = (turn * HEADS + h) % 2
                q = q_ref[:, cols]
                peak = None
                for j, (ref, r0) in enumerate(key_parts):
                    k = ref[r0 : r0 + ROWS, cols]
                    s = lax.dot_general(
                        q, k, (((1,), (1,)), ((), ())), preferred_element_type=jnp.float32
                    )
                    if masked:
                        k_ids = clip_at(
                            key_starts[j] + lax.broadcasted_iota(jnp.int32, (1, ROWS), 1), ends
                        )
                        s = jnp.where(q_ids == k_ids, s, NEG)
                    score_ref[buf, :, j * ROWS : (j + 1) * ROWS] = s
                    both = jnp.maximum(s[:, :HD], s[:, HD:])
                    peak = both if peak is None else jnp.maximum(peak, both)
                top = jnp.max(peak, axis=1, keepdims=True)
                if masked:
                    top = jnp.maximum(top, LOW)
                acc = None
                for j, (ref, r0) in enumerate(value_parts):
                    v = jnp.concatenate([ref[r0 : r0 + ROWS, cols], ones], axis=1)
                    s = score_ref[buf, :, j * ROWS : (j + 1) * ROWS]
                    w = jnp.exp2((s - top) * SCALE2).astype(jnp.bfloat16)
                    part = jnp.dot(w, v, preferred_element_type=jnp.float32)
                    acc = part if acc is None else acc + part
                total = acc[:, HD:]
                if masked:
                    total = jnp.maximum(total, 1e-30)
                out_ref[pl.ds(row0, ROWS), cols] = (acc[:, :HD] / total).astype(jnp.bfloat16)
                logs.append(top * SCALE2 + jnp.log2(total[:, :1]))
            lane = lax.broadcasted_iota(jnp.int32, (ROWS, HD), 1)
            packed = jnp.zeros((ROWS, HD), jnp.float32)
            for h in range(HEADS):
                rest = logs[h]
                for piece in range(3):
                    part = rest.astype(jnp.bfloat16).astype(jnp.float32)
                    packed = jnp.where(lane == h * 3 + piece, part, packed)
                    rest = rest - part
            out_ref[pl.ds(row0, ROWS), WIDTH:] = packed.astype(jnp.bfloat16)

    @pl.when(same)
    def _():
        body(False)

    @pl.when(jnp.logical_not(same))
    def _():
        body(True)


def combine_kernel(in_ref, out_ref):
    for m in range(8):
        stats = [in_ref[p * 8 + m, :, WIDTH:].astype(jnp.float32) for p in range(2)]
        for h in range(HEADS):
            logs = [
                s[:, 3 * h : 3 * h + 1] + s[:, 3 * h + 1 : 3 * h + 2] + s[:, 3 * h + 2 : 3 * h + 3]
                for s in stats
            ]
            top = jnp.maximum(logs[0], logs[1])
            w0 = jnp.exp2(logs[0] - top)
            w1 = jnp.exp2(logs[1] - top)
            inv = 1.0 / (w0 + w1)
            cols = slice(h * HD, (h + 1) * HD)
            a = in_ref[m, :, cols].astype(jnp.float32)
            b = in_ref[8 + m, :, cols].astype(jnp.float32)
            mixed = a * (w0 * inv) + b * (w1 * inv)
            out_ref[:, m * WIDTH + h * HD : m * WIDTH + (h + 1) * HD] = mixed.astype(jnp.bfloat16)


def shards(query, key, value, clip_lengths):
    place = jnp.stack([lax.axis_index("b"), lax.axis_index("z"), lax.axis_index("y")])
    place = place.astype(jnp.int32)
    up = [(i, (i + 1) % 8) for i in range(8)]
    down = [(i, (i - 1) % 8) for i in range(8)]
    kv = jnp.concatenate([key, value], axis=0)
    q_other = lax.ppermute(query, "z", [(0, 1), (1, 0)])
    right = left = kv
    blocks = [kv]
    for _ in range(3):
        right = lax.ppermute(right, "y", up)
        left = lax.ppermute(left, "y", down)
        blocks += [right, left]
    far_key = lax.ppermute(right[:ROWS], "y", up)
    far_value = lax.ppermute(left[ROWS:], "y", down)
    vmem = pl.BlockSpec(memory_space=pltpu.VMEM)
    smem = pl.BlockSpec(memory_space=pltpu.SMEM)
    sent = pl.pallas_call(
        attend_kernel,
        out_shape=jax.ShapeDtypeStruct((2 * ROWS, SENT), jnp.bfloat16),
        in_specs=[smem, smem] + [vmem] * 11,
        out_specs=vmem,
        scratch_shapes=[pltpu.VMEM((2, ROWS, SPAN // 2), jnp.float32)],
        compiler_params=pltpu.CompilerParams(vmem_limit_bytes=40 << 20),
        cost_estimate=pl.CostEstimate(
            flops=2 * 2 * 512 * 2048 * 128 * 3, bytes_accessed=4 << 20, transcendentals=3 << 20
        ),
    )(place, clip_lengths, query, q_other, *blocks, far_key, far_value)
    got = lax.all_to_all(
        sent.reshape(16, 32, SENT), ("z", "x", "c"), split_axis=0, concat_axis=0, tiled=True
    )
    return pl.pallas_call(
        combine_kernel,
        out_shape=jax.ShapeDtypeStruct((32, 8 * WIDTH), jnp.bfloat16),
        in_specs=[vmem],
        out_specs=vmem,
    )(got)


def solution(mesh):
    split = Mesh(mesh.devices.reshape(4, 2, 8, 4, 2), ("b", "z", "y", "x", "c"))
    part = P(("b", "z", "y"), ("x", "c"))
    return jax.shard_map(
        shards,
        mesh=split,
        in_specs=(part, part, part, P()),
        out_specs=P(("b", "z", "y", "x", "c"), None),
        check_vma=False,
    )
```

```python
import jax
import jax.numpy as jnp
from jax import lax
from jax.experimental import pallas as pl
from jax.experimental.pallas import tpu as pltpu
from jax.sharding import Mesh, PartitionSpec as P

HD = 128
HEADS = 3
ROWS = 256
SPAN = 4096
PARTS = 8
WIDTH = HEADS * HD
SENT = WIDTH + HD
SCALE2 = 1.4426950408889634 / HD**0.5
NEG = -1e30
ROOT_SCALE = 16384.0
LOW = -1e20


def clip_at(place, ends):
    return sum((place >= e).astype(jnp.int32) for e in ends)


def attend_kernel(place_ref, lengths_ref, q_own, q_other, kv_ref, out_ref, score_ref):
    bucket, z, y = place_ref[0], place_ref[1], place_ref[2]
    ends = []
    running = jnp.int32(0)
    for slot in range(3):
        running = running + lengths_ref[bucket, slot]
        ends.append(running)
    half = SPAN // 2
    key_start = z * half
    q_starts = [z * half + y * ROWS, (1 - z) * half + y * ROWS]
    first = clip_at(key_start, ends)
    same = first == clip_at(key_start + half - 1, ends)
    for q0 in q_starts:
        same &= first == clip_at(q0, ends)
        same &= first == clip_at(q0 + ROWS - 1, ends)

    def body(masked):
        ones = jnp.ones((ROWS, HD), jnp.bfloat16)
        for turn, (q_ref, q0) in enumerate(zip((q_own, q_other), q_starts)):
            row0 = pl.multiple_of((z if turn == 0 else 1 - z) * ROWS, ROWS)
            logs = []
            if masked:
                q_ids = clip_at(q0 + lax.broadcasted_iota(jnp.int32, (ROWS, 1), 0), ends)
            for h in range(HEADS):
                cols = slice(h * HD, (h + 1) * HD)
                buf = (turn * HEADS + h) % 2
                q = q_ref[:, cols]
                peak = None
                for j in range(PARTS):
                    k = kv_ref[j, 0, :, cols]
                    s = lax.dot_general(
                        q, k, (((1,), (1,)), ((), ())), preferred_element_type=jnp.float32
                    )
                    if masked:
                        k_ids = clip_at(
                            key_start + j * ROWS + lax.broadcasted_iota(jnp.int32, (1, ROWS), 1),
                            ends,
                        )
                        s = jnp.where(q_ids == k_ids, s, NEG)
                    score_ref[buf, :, j * ROWS : (j + 1) * ROWS] = s
                    both = jnp.maximum(s[:, :HD], s[:, HD:])
                    peak = both if peak is None else jnp.maximum(peak, both)
                top = jnp.max(peak, axis=1, keepdims=True)
                if masked:
                    top = jnp.maximum(top, LOW)
                acc = None
                for j in range(PARTS):
                    v = jnp.concatenate([kv_ref[j, 1, :, cols], ones], axis=1)
                    s = score_ref[buf, :, j * ROWS : (j + 1) * ROWS]
                    w = jnp.exp2((s - top) * SCALE2).astype(jnp.bfloat16)
                    part = jnp.dot(w, v, preferred_element_type=jnp.float32)
                    acc = part if acc is None else acc + part
                total = acc[:, HD:]
                if masked:
                    total = jnp.maximum(total, 1e-30)
                out_ref[pl.ds(row0, ROWS), cols] = (acc[:, :HD] / total).astype(jnp.bfloat16)
                logs.append(top * SCALE2 + jnp.log2(total[:, :1]))
            lane = lax.broadcasted_iota(jnp.int32, (ROWS, HD), 1)
            packed = jnp.zeros((ROWS, HD), jnp.float32)
            for h in range(HEADS):
                rest = logs[h]
                for piece in range(3):
                    part = rest.astype(jnp.bfloat16).astype(jnp.float32)
                    packed = jnp.where(lane == h * 3 + piece, part, packed)
                    rest = rest - part
            out_ref[pl.ds(row0, ROWS), WIDTH:] = packed.astype(jnp.bfloat16)

    @pl.when(same)
    def _():
        body(False)

    @pl.when(jnp.logical_not(same))
    def _():
        body(True)


def combine_kernel(in_ref, out_ref):
    lane = lax.broadcasted_iota(jnp.int32, (HD, WIDTH), 0)
    col = lax.broadcasted_iota(jnp.int32, (HD, WIDTH), 1)
    pick = jnp.zeros((HD, WIDTH), jnp.bool_)
    for h in range(HEADS):
        mine = (lane >= 3 * h) & (lane < 3 * h + 3) & (col >= h * HD) & (col < (h + 1) * HD)
        pick = pick | mine
    pick = jnp.where(pick, 1.0, 0.0).astype(jnp.bfloat16)
    for m in range(8):
        log0 = jnp.dot(in_ref[m, :, WIDTH:], pick, preferred_element_type=jnp.float32)
        log1 = jnp.dot(in_ref[8 + m, :, WIDTH:], pick, preferred_element_type=jnp.float32)
        share = 1.0 / (1.0 + jnp.exp2(log0 - log1))
        a = in_ref[m, :, :WIDTH].astype(jnp.float32)
        b = in_ref[8 + m, :, :WIDTH].astype(jnp.float32)
        out_ref[:, m * WIDTH : (m + 1) * WIDTH] = (a + (b - a) * share).astype(jnp.bfloat16)


def shards(query, key, value, clip_lengths):
    place = jnp.stack([lax.axis_index("b"), lax.axis_index("z"), lax.axis_index("y")])
    place = place.astype(jnp.int32)
    q_other = lax.ppermute(query, "z", [(0, 1), (1, 0)])
    kv = jnp.concatenate([key, value], axis=0).astype(jnp.float32)
    sent_kv = (jnp.sign(kv) * jnp.sqrt(jnp.abs(kv)) * ROOT_SCALE).astype(jnp.float16)
    got_kv = lax.all_gather(sent_kv, "y", axis=0, tiled=True).astype(jnp.float32)
    kv_all = (got_kv * jnp.abs(got_kv) * (1.0 / ROOT_SCALE**2)).astype(jnp.bfloat16)
    vmem = pl.BlockSpec(memory_space=pltpu.VMEM)
    smem = pl.BlockSpec(memory_space=pltpu.SMEM)
    sent = pl.pallas_call(
        attend_kernel,
        out_shape=jax.ShapeDtypeStruct((2 * ROWS, SENT), jnp.bfloat16),
        in_specs=[smem, smem] + [vmem] * 3,
        out_specs=vmem,
        scratch_shapes=[pltpu.VMEM((2, ROWS, SPAN // 2), jnp.float32)],
        compiler_params=pltpu.CompilerParams(vmem_limit_bytes=40 << 20),
        cost_estimate=pl.CostEstimate(
            flops=2 * 2 * 512 * 2048 * 128 * 3, bytes_accessed=4 << 20, transcendentals=3 << 20
        ),
    )(place, clip_lengths, query, q_other, kv_all.reshape(PARTS, 2, ROWS, WIDTH))
    got = lax.all_to_all(
        sent.reshape(16, 32, SENT), ("z", "x", "c"), split_axis=0, concat_axis=0, tiled=True
    )
    return pl.pallas_call(
        combine_kernel,
        out_shape=jax.ShapeDtypeStruct((32, 8 * WIDTH), jnp.bfloat16),
        in_specs=[vmem],
        out_specs=vmem,
    )(got)


def solution(mesh):
    split = Mesh(mesh.devices.reshape(4, 2, 8, 4, 2), ("b", "z", "y", "x", "c"))
    part = P(("b", "z", "y"), ("x", "c"))
    return jax.shard_map(
        shards,
        mesh=split,
        in_specs=(part, part, part, P()),
        out_specs=P(("b", "z", "y", "x", "c"), None),
        check_vma=False,
    )
```

```python
import jax
import jax.numpy as jnp
from jax import lax
from jax.experimental import pallas as pl
from jax.experimental.pallas import tpu as pltpu
from jax.sharding import Mesh, PartitionSpec as P

HD = 128
HEADS = 3
ROWS = 256
SPAN = 4096
PARTS = 8
WIDTH = HEADS * HD
SENT = WIDTH + HD
SCALE2 = 1.4426950408889634 / HD**0.5
NEG = -1e30
ROOT_SCALE = 16384.0
LOW = -1e20


def clip_at(place, ends):
    return sum((place >= e).astype(jnp.int32) for e in ends)


def attend_kernel(place_ref, lengths_ref, q_own, q_other, kv_ref, out_ref, score_ref):
    bucket, z, y = place_ref[0], place_ref[1], place_ref[2]
    ends = []
    running = jnp.int32(0)
    for slot in range(3):
        running = running + lengths_ref[bucket, slot]
        ends.append(running)
    half = SPAN // 2
    key_start = z * half
    q_starts = [z * half + y * ROWS, (1 - z) * half + y * ROWS]
    first = clip_at(key_start, ends)
    same = first == clip_at(key_start + half - 1, ends)
    for q0 in q_starts:
        same &= first == clip_at(q0, ends)
        same &= first == clip_at(q0 + ROWS - 1, ends)

    def body(masked):
        ones = jnp.ones((ROWS, HD), jnp.bfloat16)
        tiles = [(turn, h) for turn in range(2) for h in range(HEADS)]
        q_ids = []
        if masked:
            rows = lax.broadcasted_iota(jnp.int32, (ROWS, 1), 0)
            q_ids = [clip_at(q0 + rows, ends) for q0 in q_starts]
        tops, logs = [], []
        for i in range(len(tiles) + 1):
            peak = acc = None
            for j in range(PARTS):
                part = slice(j * ROWS, (j + 1) * ROWS)
                if i < len(tiles):
                    turn, h = tiles[i]
                    cols = slice(h * HD, (h + 1) * HD)
                    s = lax.dot_general(
                        (q_own, q_other)[turn][:, cols],
                        kv_ref[j, 0, :, cols],
                        (((1,), (1,)), ((), ())),
                        preferred_element_type=jnp.float32,
                    )
                    if masked:
                        lanes = lax.broadcasted_iota(jnp.int32, (1, ROWS), 1)
                        k_ids = clip_at(key_start + j * ROWS + lanes, ends)
                        s = jnp.where(q_ids[turn] == k_ids, s, NEG)
                    score_ref[i % 2, :, part] = s
                    both = jnp.maximum(s[:, :HD], s[:, HD:])
                    peak = both if peak is None else jnp.maximum(peak, both)
                if i > 0:
                    turn, h = tiles[i - 1]
                    cols = slice(h * HD, (h + 1) * HD)
                    v = jnp.concatenate([kv_ref[j, 1, :, cols], ones], axis=1)
                    s = score_ref[(i - 1) % 2, :, part]
                    w = jnp.exp2((s - tops[i - 1]) * SCALE2).astype(jnp.bfloat16)
                    more = jnp.dot(w, v, preferred_element_type=jnp.float32)
                    acc = more if acc is None else acc + more
            if i < len(tiles):
                top = jnp.max(peak, axis=1, keepdims=True)
                tops.append(jnp.maximum(top, LOW) if masked else top)
            if i > 0:
                turn, h = tiles[i - 1]
                row0 = pl.multiple_of((z if turn == 0 else 1 - z) * ROWS, ROWS)
                total = acc[:, HD:]
                if masked:
                    total = jnp.maximum(total, 1e-30)
                out_ref[pl.ds(row0, ROWS), h * HD : (h + 1) * HD] = (acc[:, :HD] / total).astype(
                    jnp.bfloat16
                )
                logs.append(tops[i - 1] * SCALE2 + jnp.log2(total[:, :1]))
                if h == HEADS - 1:
                    lane = lax.broadcasted_iota(jnp.int32, (ROWS, HD), 1)
                    packed = jnp.zeros((ROWS, HD), jnp.float32)
                    for hh in range(HEADS):
                        rest = logs[turn * HEADS + hh]
                        for piece in range(3):
                            high = rest.astype(jnp.bfloat16).astype(jnp.float32)
                            packed = jnp.where(lane == hh * 3 + piece, high, packed)
                            rest = rest - high
                    out_ref[pl.ds(row0, ROWS), WIDTH:] = packed.astype(jnp.bfloat16)

    @pl.when(same)
    def _():
        body(False)

    @pl.when(jnp.logical_not(same))
    def _():
        body(True)


def combine_kernel(in_ref, out_ref):
    lane = lax.broadcasted_iota(jnp.int32, (HD, WIDTH), 0)
    col = lax.broadcasted_iota(jnp.int32, (HD, WIDTH), 1)
    pick = jnp.zeros((HD, WIDTH), jnp.bool_)
    for h in range(HEADS):
        mine = (lane >= 3 * h) & (lane < 3 * h + 3) & (col >= h * HD) & (col < (h + 1) * HD)
        pick = pick | mine
    pick = jnp.where(pick, 1.0, 0.0).astype(jnp.bfloat16)
    for m in range(8):
        log0 = jnp.dot(in_ref[m, :, WIDTH:], pick, preferred_element_type=jnp.float32)
        log1 = jnp.dot(in_ref[8 + m, :, WIDTH:], pick, preferred_element_type=jnp.float32)
        share = 1.0 / (1.0 + jnp.exp2(log0 - log1))
        a = in_ref[m, :, :WIDTH].astype(jnp.float32)
        b = in_ref[8 + m, :, :WIDTH].astype(jnp.float32)
        out_ref[:, m * WIDTH : (m + 1) * WIDTH] = (a + (b - a) * share).astype(jnp.bfloat16)


def shards(query, key, value, clip_lengths):
    place = jnp.stack([lax.axis_index("b"), lax.axis_index("z"), lax.axis_index("y")])
    place = place.astype(jnp.int32)
    q_other = lax.ppermute(query, "z", [(0, 1), (1, 0)])
    kv = jnp.concatenate([key, value], axis=0).astype(jnp.float32)
    sent_kv = (jnp.sign(kv) * jnp.sqrt(jnp.abs(kv)) * ROOT_SCALE).astype(jnp.float16)
    got_kv = lax.all_gather(sent_kv, "y", axis=0, tiled=True).astype(jnp.float32)
    kv_all = (got_kv * jnp.abs(got_kv) * (1.0 / ROOT_SCALE**2)).astype(jnp.bfloat16)
    vmem = pl.BlockSpec(memory_space=pltpu.VMEM)
    smem = pl.BlockSpec(memory_space=pltpu.SMEM)
    sent = pl.pallas_call(
        attend_kernel,
        out_shape=jax.ShapeDtypeStruct((2 * ROWS, SENT), jnp.bfloat16),
        in_specs=[smem, smem] + [vmem] * 3,
        out_specs=vmem,
        scratch_shapes=[pltpu.VMEM((2, ROWS, SPAN // 2), jnp.float32)],
        compiler_params=pltpu.CompilerParams(vmem_limit_bytes=40 << 20),
        cost_estimate=pl.CostEstimate(
            flops=2 * 2 * 512 * 2048 * 128 * 3, bytes_accessed=4 << 20, transcendentals=3 << 20
        ),
    )(place, clip_lengths, query, q_other, kv_all.reshape(PARTS, 2, ROWS, WIDTH))
    got = lax.all_to_all(
        sent.reshape(16, 32, SENT), ("z", "x", "c"), split_axis=0, concat_axis=0, tiled=True
    )
    return pl.pallas_call(
        combine_kernel,
        out_shape=jax.ShapeDtypeStruct((32, 8 * WIDTH), jnp.bfloat16),
        in_specs=[vmem],
        out_specs=vmem,
        compiler_params=pltpu.CompilerParams(vmem_limit_bytes=4 << 20),
    )(got)


def solution(mesh):
    split = Mesh(mesh.devices.reshape(4, 2, 8, 4, 2), ("b", "z", "y", "x", "c"))
    part = P(("b", "z", "y"), ("x", "c"))
    return jax.shard_map(
        shards,
        mesh=split,
        in_specs=(part, part, part, P()),
        out_specs=P(("b", "z", "y", "x", "c"), None),
        check_vma=False,
    )
```

```python
import jax
import jax.numpy as jnp
from jax import lax
from jax.experimental import pallas as pl
from jax.experimental.pallas import tpu as pltpu
from jax.sharding import Mesh, PartitionSpec as P

HD = 128
HEADS = 3
ROWS = 256
SPAN = 4096
PARTS = 8
WIDTH = HEADS * HD
CHUNK = 32
SENT = WIDTH // HD * CHUNK + 8
SCALE2 = 1.4426950408889634 / HD**0.5
NEG = -1e30
ROOT_SCALE = 16384.0
LOW = -1e20


def clip_at(place, ends):
    return sum((place >= e).astype(jnp.int32) for e in ends)


def attend_kernel(place_ref, lengths_ref, q_own, q_other, kv_ref, out_ref, score_ref):
    bucket, z, y = place_ref[0], place_ref[1], place_ref[2]
    ends = []
    running = jnp.int32(0)
    for slot in range(3):
        running = running + lengths_ref[bucket, slot]
        ends.append(running)
    half = SPAN // 2
    key_start = z * half
    q_starts = [z * half + y * ROWS, (1 - z) * half + y * ROWS]
    first = clip_at(key_start, ends)
    same = first == clip_at(key_start + half - 1, ends)
    for q0 in q_starts:
        same &= first == clip_at(q0, ends)
        same &= first == clip_at(q0 + ROWS - 1, ends)

    def body(masked):
        ones = jnp.ones((ROWS, HD), jnp.bfloat16)
        tiles = [(turn, h) for turn in range(2) for h in range(HEADS)]
        q_ids = []
        if masked:
            rows = lax.broadcasted_iota(jnp.int32, (ROWS, 1), 0)
            q_ids = [clip_at(q0 + rows, ends) for q0 in q_starts]
        tops, logs = [], []
        for i in range(len(tiles) + 1):
            peak = acc = None
            for j in range(PARTS):
                part = slice(j * ROWS, (j + 1) * ROWS)
                if i < len(tiles):
                    turn, h = tiles[i]
                    cols = slice(h * HD, (h + 1) * HD)
                    s = lax.dot_general(
                        (q_own, q_other)[turn][:, cols],
                        kv_ref[j, 0, :, cols],
                        (((1,), (1,)), ((), ())),
                        preferred_element_type=jnp.float32,
                    )
                    if masked:
                        lanes = lax.broadcasted_iota(jnp.int32, (1, ROWS), 1)
                        k_ids = clip_at(key_start + j * ROWS + lanes, ends)
                        s = jnp.where(q_ids[turn] == k_ids, s, NEG)
                    score_ref[i % 2, :, part] = s
                    both = jnp.maximum(s[:, :HD], s[:, HD:])
                    peak = both if peak is None else jnp.maximum(peak, both)
                if i > 0:
                    turn, h = tiles[i - 1]
                    cols = slice(h * HD, (h + 1) * HD)
                    v = jnp.concatenate([kv_ref[j, 1, :, cols], ones], axis=1)
                    s = score_ref[(i - 1) % 2, :, part]
                    w = jnp.exp2((s - tops[i - 1]) * SCALE2).astype(jnp.bfloat16)
                    more = jnp.dot(w, v, preferred_element_type=jnp.float32)
                    acc = more if acc is None else acc + more
            if i < len(tiles):
                top = jnp.max(peak, axis=1, keepdims=True)
                tops.append(jnp.maximum(top, LOW) if masked else top)
            if i > 0:
                turn, h = tiles[i - 1]
                side = z if turn == 0 else 1 - z
                total = acc[:, HD:]
                if masked:
                    total = jnp.maximum(total, 1e-30)
                mean = (acc[:, :HD] / total).astype(jnp.bfloat16)
                for m in range(8):
                    out_ref[2 * m + side, h * CHUNK : (h + 1) * CHUNK, :] = mean[
                        m * CHUNK : (m + 1) * CHUNK
                    ]
                logs.append(tops[i - 1] * SCALE2 + jnp.log2(total[:, :1]))
                if h == HEADS - 1:
                    lane = lax.broadcasted_iota(jnp.int32, (ROWS, HD), 1)
                    packed = jnp.zeros((ROWS, HD), jnp.float32)
                    for hh in range(HEADS):
                        rest = logs[turn * HEADS + hh]
                        for piece in range(3):
                            high = rest.astype(jnp.bfloat16).astype(jnp.float32)
                            packed = jnp.where(lane == hh * 3 + piece, high, packed)
                            rest = rest - high
                    for m in range(8):
                        tile = packed[m * CHUNK : m * CHUNK + 8]
                        for g in range(1, 4):
                            rows8 = packed[m * CHUNK + 8 * g : m * CHUNK + 8 * g + 8]
                            tile = tile + pltpu.roll(rows8, 16 * g, 1)
                        out_ref[2 * m + side, HEADS * CHUNK :, :] = tile.astype(jnp.bfloat16)

    @pl.when(same)
    def _():
        body(False)

    @pl.when(jnp.logical_not(same))
    def _():
        body(True)


def combine_kernel(in_ref, out_ref):
    tiles = in_ref[:, HEADS * CHUNK :, :].astype(jnp.float32).reshape(128, HD)
    tiles = tiles.astype(jnp.bfloat16)
    lane = lax.broadcasted_iota(jnp.int32, (HD, WIDTH), 0)
    head = lax.broadcasted_iota(jnp.int32, (HD, WIDTH), 1) // HD
    shares = []
    for g in range(4):
        low = 16 * g + 3 * head
        pick = jnp.where((lane >= low) & (lane < low + 3), 1.0, 0.0).astype(jnp.bfloat16)
        shares.append(jnp.dot(tiles, pick, preferred_element_type=jnp.float32))
    for m in range(8):
        logs = [
            jnp.concatenate([s[8 * (2 * m + p) : 8 * (2 * m + p) + 8] for s in shares], axis=0)
            for p in range(2)
        ]
        share = 1.0 / (1.0 + jnp.exp2(logs[0] - logs[1]))
        for h in range(HEADS):
            a = in_ref[2 * m, h * CHUNK : (h + 1) * CHUNK, :].astype(jnp.float32)
            b = in_ref[2 * m + 1, h * CHUNK : (h + 1) * CHUNK, :].astype(jnp.float32)
            mixed = a + (b - a) * share[:, h * HD : (h + 1) * HD]
            out_ref[:, m * WIDTH + h * HD : m * WIDTH + (h + 1) * HD] = mixed.astype(jnp.bfloat16)


def shards(query, key, value, clip_lengths):
    place = jnp.stack([lax.axis_index("b"), lax.axis_index("z"), lax.axis_index("y")])
    place = place.astype(jnp.int32)
    q_other = lax.ppermute(query, "z", [(0, 1), (1, 0)])
    kv = jnp.concatenate([key, value], axis=0).astype(jnp.float32)
    sent_kv = (kv * lax.rsqrt(jnp.maximum(jnp.abs(kv), 1e-36)) * ROOT_SCALE).astype(jnp.float16)
    got_kv = lax.all_gather(sent_kv, "y", axis=0, tiled=True).astype(jnp.float32)
    kv_all = (got_kv * jnp.abs(got_kv) * (1.0 / ROOT_SCALE**2)).astype(jnp.bfloat16)
    vmem = pl.BlockSpec(memory_space=pltpu.VMEM)
    smem = pl.BlockSpec(memory_space=pltpu.SMEM)
    sent = pl.pallas_call(
        attend_kernel,
        out_shape=jax.ShapeDtypeStruct((16, SENT, HD), jnp.bfloat16),
        in_specs=[smem, smem] + [vmem] * 3,
        out_specs=vmem,
        scratch_shapes=[pltpu.VMEM((2, ROWS, SPAN // 2), jnp.float32)],
        compiler_params=pltpu.CompilerParams(vmem_limit_bytes=40 << 20),
        cost_estimate=pl.CostEstimate(
            flops=2 * 2 * 512 * 2048 * 128 * 3, bytes_accessed=4 << 20, transcendentals=3 << 20
        ),
    )(place, clip_lengths, query, q_other, kv_all.reshape(PARTS, 2, ROWS, WIDTH))
    got = lax.all_to_all(sent, ("x", "c", "z"), split_axis=0, concat_axis=0, tiled=True)
    return pl.pallas_call(
        combine_kernel,
        out_shape=jax.ShapeDtypeStruct((32, 8 * WIDTH), jnp.bfloat16),
        in_specs=[vmem],
        out_specs=vmem,
        compiler_params=pltpu.CompilerParams(vmem_limit_bytes=4 << 20),
    )(got)


def solution(mesh):
    split = Mesh(mesh.devices.reshape(4, 2, 8, 4, 2), ("b", "z", "y", "x", "c"))
    part = P(("b", "z", "y"), ("x", "c"))
    return jax.shard_map(
        shards,
        mesh=split,
        in_specs=(part, part, part, P()),
        out_specs=P(("b", "z", "y", "x", "c"), None),
        check_vma=False,
    )
```
